32 devices in a mesh: grp: 2 (over y), seq: 4 (over x, core), sub: 4 (over z).
Axes of the slice: x: 2, y: 2, z: 4, core: 2. Of those that a mesh axis runs over, the one named last changes fastest.
Arguments:
- events: bfloat16 [4096, 1024], P(('grp', 'seq', 'sub')), parts along dimension 0, may hold values from -36 to 36
- offsets: int32 [4096], P(('grp', 'seq', 'sub')), parts along dimension 0, may hold values from 0 to 2047
- cotangent: bfloat16 [4096, 1024], P(('grp', 'seq', 'sub')), parts along dimension 0, may hold values from -6 to 6
- query_weight: bfloat16 [1024, 1024], P('sub'), may hold values from -0.1875 to 0.1875
- key_weight: bfloat16 [1024, 1024], P('sub'), may hold values from -0.1875 to 0.1875
- value_weight: bfloat16 [1024, 1024], P('sub'), may hold values from -0.1875 to 0.1875
- omega: bfloat16 [8, 128, 256], replicated, may hold values from -0.5 to 0.5
Outputs:
- grad_events: bfloat16 [4096, 1024], P(('grp', 'seq', 'sub')), parts along dimension 0
The draws below stay inside these ranges and needn't reach their ends.
There are 2 independent parts, one for each index of `grp`. The reference program is written for one: setup_inputs(seed, part) draws one part's arguments, and reference() takes and returns one part's arrays. A program takes and returns all parts, laid end to end along the dimension named above; an argument that names none is the same for every part. Nothing has to cross between parts.
All inputs are finite; a program needn't handle non-finite values.
Results may differ from the reference program's by a relative error of at most 0.012.
Values may be sent and summed in bfloat16 or wider, within the bound.
A program may use at most 64 MiB of HBM per device.

```python
import math
import jax
import jax.numpy as jnp
from jax import lax

D = 1024
H = 8
M = 256
TOK_DEV = 128
HD = 128
TOKENS = 2048
N_SUB = 4


def draw_events(key, part):
    block_count = TOKENS // TOK_DEV
    ranks = jax.random.permutation(jax.random.fold_in(key, 11), block_count).astype(jnp.float32)
    scales = 0.5 * jnp.exp(ranks / max(block_count - 1, 1) * jnp.log(12.0))
    noise_key = jax.random.fold_in(key, 12)
    noise = jnp.clip(jax.random.normal(noise_key, (block_count, TOK_DEV, D), jnp.float32), -6.0, 6.0)
    values = noise * scales[:, None, None]
    return values.reshape(TOKENS, D).astype(jnp.bfloat16)


def plant(array, stream_key, smallest, top_value):
    longest = array.shape.index(max(array.shape))
    spots = []
    for shift in (0, 1):
        where = [jax.random.randint(jax.random.fold_in(stream_key, axis), (), 0, length) for axis, length in enumerate(array.shape)]
        where[longest] = (where[longest] + shift) % array.shape[longest]
        spots.append(tuple(where))
    return array.at[spots[0]].set(smallest).at[spots[1]].set(top_value)


def levels(rng, extent, split, least, high):
    def one(axis_at, blocks):
        draws = jax.random.uniform(jax.random.fold_in(jax.random.fold_in(rng, 6), axis_at), (blocks,), jnp.float32, least / len(split), high / len(split))
        return jnp.repeat(jnp.exp(draws), extent[axis_at] // blocks).reshape((-1,) + (1,) * (len(extent) - axis_at - 1))

    factor_of = one(*split[0])
    for cut in split[1:]:
        factor_of = factor_of * one(*cut)
    return factor_of


def bell_draw(rng, extent, spread, reach, pieces=(), held_as=jnp.bfloat16):
    entries = spread * jax.random.normal(rng, extent, jnp.float32)
    if pieces:
        entries = entries * levels(rng, extent, pieces, -0.22, 0.18)
    return jnp.clip(entries, -reach, reach).astype(held_as)


def setup_inputs(seed: int = 0, part: int = 0) -> dict:
    keys = jax.random.split(jax.random.key(seed), 8)
    own_keys = jax.random.split(jax.random.fold_in(keys[7], part), 8)
    return {
        "events": draw_events(jax.random.fold_in(jax.random.fold_in(keys[7], part), 71), part),
        "offsets": plant(jax.random.randint(own_keys[1], (TOKENS,), 0, 2048), jax.random.fold_in(own_keys[1], 1), 0, 2047).astype(jnp.int32),
        "cotangent": bell_draw(own_keys[2], (TOKENS, D), 1.0, 6.0, ((0, 16),)),
        "query_weight": bell_draw(keys[3], (D, D), D ** -0.5, 0.1875, ((0, 4),)),
        "key_weight": bell_draw(keys[4], (D, D), D ** -0.5, 0.1875, ((0, 4),)),
        "value_weight": bell_draw(keys[5], (D, D), D ** -0.5, 0.1875, ((0, 4),)),
        "omega": bell_draw(keys[6], (H, HD, M), HD ** -0.5, 0.5),
    }


def encode(events, offsets):
    half_width = events.shape[1] // 2
    indices = jnp.arange(half_width, dtype=jnp.float32)
    frequency = jnp.exp(indices * (-2.0 * math.log(10000.0) / events.shape[1]))
    angles = offsets.astype(jnp.float32)[:, None] * frequency[None, :]
    encoding = jnp.concatenate([jnp.sin(angles), jnp.cos(angles)], axis=1)
    return (events.astype(jnp.float32) + encoding).astype(jnp.bfloat16)

def project(inputs, weight):
    return jnp.dot(inputs, weight, preferred_element_type=jnp.float32).astype(jnp.bfloat16)

def reference(events, offsets, cotangent, query_weight, key_weight, value_weight, omega):
    widened_rows = jnp.float32
    inputs = encode(events, offsets)
    queries = project(inputs, query_weight)
    key_act = project(inputs, key_weight)
    value_act = project(inputs, value_weight)
    block_rows = TOK_DEV * N_SUB
    block_count = TOKENS // block_rows
    omega_wide = omega.astype(widened_rows)
    loss_scale = math.sqrt(TOKENS)

    def as_blocks(matrix):
        return matrix.reshape(block_count, block_rows, H, D // H)

    def featurize(acts):
        pre_act = jnp.einsum('thd,hdm->thm', acts.astype(widened_rows), omega_wide)
        return (pre_act, jax.nn.softplus(pre_act).astype(jnp.bfloat16))

    def add_keys(running_state, block_pair):
        key_blk, value_block = block_pair
        _, key_feature_map = featurize(key_blk)
        key_widened = key_feature_map.astype(widened_rows)
        state_digest = running_state[0] + jnp.einsum('reb,rec->ebc', key_widened, value_block.astype(widened_rows))
        return ((state_digest, running_state[1] + lax.optimization_barrier(jnp.sum(key_widened, axis=0))), None)
    starting = (jnp.zeros((H, M, D // H), widened_rows), jnp.zeros((H, M), widened_rows))
    (state_digest, key_total), _ = lax.scan(add_keys, starting, (as_blocks(key_act), as_blocks(value_act)))
    digest_halves = state_digest.astype(jnp.bfloat16)
    total_half = key_total.astype(jnp.bfloat16)

    def query_side(query_blk, upstream_blk):
        query_pre, query_feature_map = featurize(query_blk)
        query_widened = query_feature_map.astype(widened_rows)
        numerator = jnp.einsum('xls,lsk->xlk', query_widened, digest_halves.astype(widened_rows))
        denom = jnp.einsum('thm,hm->th', query_widened, total_half.astype(widened_rows))
        attended = numerator / denom[..., None]
        upstream = upstream_blk.astype(widened_rows) * loss_scale
        scaled_grad = upstream / denom[..., None]
        norm_grad = -lax.optimization_barrier(jnp.sum(scaled_grad * attended, axis=-1))
        return (query_pre, query_feature_map, scaled_grad.astype(jnp.bfloat16), norm_grad, norm_grad.astype(jnp.bfloat16))

    def add_queries(running_state, block_pair):
        _, query_feature_map, scaled_halves, _, norm_half = query_side(block_pair[0], block_pair[1])
        query_widened = query_feature_map.astype(widened_rows)
        gradient_summed = running_state[0] + jnp.einsum('reb,rec->ebc', query_widened, scaled_halves.astype(widened_rows))
        total_sum = running_state[1] + jnp.einsum('thm,th->hm', query_widened, norm_half.astype(widened_rows))
        return ((gradient_summed, total_sum), None)
    query_blocks = as_blocks(queries)
    upstream_blocks = as_blocks(cotangent)
    (summary_grad, overall_gradient), _ = lax.scan(add_queries, starting, (query_blocks, upstream_blocks))
    gradient_halves = summary_grad.astype(jnp.bfloat16).astype(widened_rows)

    def gradients(block_set):
        query_blk, key_blk, value_block, upstream_blk = block_set
        query_pre, _, scaled_halves, norm_grad, _ = query_side(query_blk, upstream_blk)
        key_pre, key_feature_map = featurize(key_blk)
        query_feature_gradient = jnp.einsum('pfy,fly->pfl', scaled_halves.astype(widened_rows), digest_halves.astype(widened_rows))
        query_feature_gradient = query_feature_gradient + norm_grad[..., None] * total_half.astype(widened_rows)[None]
        key_feature_gradient = jnp.einsum('pfy,fly->pfl', value_block.astype(widened_rows), gradient_halves) + overall_gradient[None]
        value_gradient = jnp.einsum('xls,lsk->xlk', key_feature_map.astype(widened_rows), gradient_halves).astype(jnp.bfloat16)
        query_pre_grad = (query_feature_gradient * jax.nn.sigmoid(query_pre)).astype(jnp.bfloat16)
        key_pre_grad = (key_feature_gradient * jax.nn.sigmoid(key_pre)).astype(jnp.bfloat16)
        query_grad = jnp.einsum('thm,hdm->thd', query_pre_grad.astype(widened_rows), omega_wide).astype(jnp.bfloat16)
        key_grad = jnp.einsum('thm,hdm->thd', key_pre_grad.astype(widened_rows), omega_wide).astype(jnp.bfloat16)
        return (query_grad, key_grad, value_gradient)
    query_grad, key_grad, value_gradient = lax.map(gradients, (query_blocks, as_blocks(key_act), as_blocks(value_act), upstream_blocks))
    total = jnp.dot(query_grad.reshape(TOKENS, D), query_weight.T, preferred_element_type=jnp.float32)
    total = total + jnp.dot(key_grad.reshape(TOKENS, D), key_weight.T, preferred_element_type=jnp.float32)
    total = total + jnp.dot(value_gradient.reshape(TOKENS, D), value_weight.T, preferred_element_type=jnp.float32)
    return total.astype(jnp.bfloat16)
```

```python
import functools
import math

import jax
import jax.numpy as jnp
from jax import lax
from jax.experimental import pallas as pl
from jax.experimental.pallas import tpu as pltpu
from jax.sharding import PartitionSpec as P


def encode(events, offsets):
    half_width = events.shape[1] // 2
    indices = jnp.arange(half_width, dtype=jnp.float32)
    frequency = jnp.exp(indices * (-2.0 * math.log(10000.0) / events.shape[1]))
    angles = offsets.astype(jnp.float32)[:, None] * frequency[None, :]
    encoding = jnp.concatenate([jnp.sin(angles), jnp.cos(angles)], axis=1)
    return (events.astype(jnp.float32) + encoding).astype(jnp.bfloat16)


def split_heads(matrix, head_count):
    return matrix.reshape(matrix.shape[0], head_count, matrix.shape[1] // head_count)


def transposed(left, weight):
    return lax.dot_general(
        left, weight, (((1,), (1,)), ((), ())), preferred_element_type=jnp.float32
    )


def local(events, offsets, cotangent, query_weight, key_weight, value_weight, omega):
    widened_rows = jnp.float32
    head_count = omega.shape[0]
    local_rows = events.shape[0]
    model_width = events.shape[1]
    all_tokens = local_rows * lax.axis_size("seq") * lax.axis_size("sub")
    loss_scale = math.sqrt(all_tokens)
    inputs = encode(events, offsets)
    gathered = (
        lax.all_gather(query_weight, "sub", axis=0, tiled=True),
        lax.all_gather(key_weight, "sub", axis=0, tiled=True),
        lax.all_gather(value_weight, "sub", axis=0, tiled=True),
    )
    queries, key_act, value_act = [
        jnp.dot(inputs, weight, preferred_element_type=widened_rows).astype(jnp.bfloat16)
        for weight in gathered
    ]
    query_pre = jnp.einsum(
        "thd,hdm->thm", split_heads(queries, head_count), omega, preferred_element_type=widened_rows
    )
    key_pre = jnp.einsum(
        "thd,hdm->thm", split_heads(key_act, head_count), omega, preferred_element_type=widened_rows
    )
    query_feature_map = jax.nn.softplus(query_pre).astype(jnp.bfloat16)
    key_feature_map = jax.nn.softplus(key_pre).astype(jnp.bfloat16)
    value_per_head = split_heads(value_act, head_count)
    local_digest = jnp.einsum(
        "reb,rec->ebc", key_feature_map, value_per_head, preferred_element_type=widened_rows
    )
    local_total = jnp.sum(key_feature_map, axis=0, dtype=widened_rows)
    state_digest, key_total = lax.psum((local_digest, local_total), ("seq", "sub"))
    digest_halves = state_digest.astype(jnp.bfloat16)
    total_half = key_total.astype(jnp.bfloat16)
    numerator = jnp.einsum(
        "xls,lsk->xlk", query_feature_map, digest_halves, preferred_element_type=widened_rows
    )
    denom = jnp.einsum(
        "thm,hm->th", query_feature_map, total_half, preferred_element_type=widened_rows
    )
    attended = numerator / denom[..., None]
    upstream = split_heads(cotangent, head_count).astype(widened_rows) * loss_scale
    scaled_grad = upstream / denom[..., None]
    norm_grad = -jnp.sum(scaled_grad * attended, axis=-1)
    scaled_halves = scaled_grad.astype(jnp.bfloat16)
    norm_half = norm_grad.astype(jnp.bfloat16)
    local_gradient = jnp.einsum(
        "reb,rec->ebc", query_feature_map, scaled_halves, preferred_element_type=widened_rows
    )
    local_norm = jnp.einsum(
        "thm,th->hm", query_feature_map, norm_half, preferred_element_type=widened_rows
    )
    summary_grad, overall_gradient = lax.psum((local_gradient, local_norm), ("seq", "sub"))
    gradient_halves = summary_grad.astype(jnp.bfloat16)
    query_feature_gradient = jnp.einsum(
        "pfy,fly->pfl", scaled_halves, digest_halves, preferred_element_type=widened_rows
    )
    query_feature_gradient = (
        query_feature_gradient + norm_grad[..., None] * total_half.astype(widened_rows)[None]
    )
    key_feature_gradient = (
        jnp.einsum(
            "pfy,fly->pfl", value_per_head, gradient_halves, preferred_element_type=widened_rows
        )
        + overall_gradient[None]
    )
    value_gradient = jnp.einsum(
        "xls,lsk->xlk", key_feature_map, gradient_halves, preferred_element_type=widened_rows
    ).astype(jnp.bfloat16)
    query_pre_grad = (query_feature_gradient * jax.nn.sigmoid(query_pre)).astype(jnp.bfloat16)
    key_pre_grad = (key_feature_gradient * jax.nn.sigmoid(key_pre)).astype(jnp.bfloat16)
    query_grad = jnp.einsum(
        "thm,hdm->thd", query_pre_grad, omega, preferred_element_type=widened_rows
    ).astype(jnp.bfloat16)
    key_grad = jnp.einsum(
        "thm,hdm->thd", key_pre_grad, omega, preferred_element_type=widened_rows
    ).astype(jnp.bfloat16)
    query_flat = query_grad.reshape(local_rows, model_width)
    key_flat = key_grad.reshape(local_rows, model_width)
    value_flat = value_gradient.reshape(local_rows, model_width)
    summed = transposed(query_flat, gathered[0])
    summed = summed + transposed(key_flat, gathered[1])
    summed = summed + transposed(value_flat, gathered[2])
    return summed.astype(jnp.bfloat16)


F32, BF16 = jnp.float32, jnp.bfloat16
MESH = pl.DeviceIdType.MESH
NN = (((1,), (0,)), ((), ()))
NT = (((1,), (1,)), ((), ()))
TN = (((0,), (0,)), ((), ()))


def mul(left, right, dims):
    return lax.dot_general(left, right, dims, preferred_element_type=F32)


def activations(pre):
    small = jnp.exp(-jnp.abs(pre))
    feature = jnp.maximum(pre, 0.0) + jnp.log1p(small)
    sigmoid = jnp.where(pre >= 0.0, 1.0, small) / (1.0 + small)
    return feature.astype(BF16), sigmoid


def kernel(
    n_grp, n_seq, n_sub, loss_scale,
    x_ref, cot_ref, wq_ref, wk_ref, wv_ref, omega_ref, out_ref,
    xall, call, wall, om, qf, kf, qs, ks, va, sc, nrm, gr,
    acc, part, rsin, half, tot, totin, ob, oin,
    local_sem, xs, xr, cs, cr, ws, wr, ss, sr, osend, orecv,
):
    planes = n_grp * n_seq
    grp, seq, sub = lax.axis_index("grp"), lax.axis_index("seq"), lax.axis_index("sub")
    me = grp * n_seq + seq
    block, width = x_ref.shape
    head = om.shape[0]
    rows = wq_ref.shape[0]
    record = n_seq * block
    piece = n_grp * head // n_sub

    def in_plane(index):
        return {"grp": index // n_seq, "seq": index % n_seq, "sub": sub}

    def in_column(index):
        return {"grp": grp, "seq": seq, "sub": index}

    def rows_of(index, size):
        return pl.ds(pl.multiple_of(index * size, size), size)

    def lanes(index):
        return pl.ds(pl.multiple_of(index * head, head), head)

    def remote(src, dst, send, recv, device):
        return pltpu.make_async_remote_copy(
            src_ref=src, dst_ref=dst, send_sem=send, recv_sem=recv, device_id=device, device_id_type=MESH
        )

    barrier = pltpu.get_barrier_semaphore()
    for d in range(1, planes):
        pl.semaphore_signal(barrier, inc=1, device_id=in_plane((me + d) % planes), device_id_type=MESH)
    for d in range(1, n_sub):
        pl.semaphore_signal(barrier, inc=1, device_id=in_column((sub + d) % n_sub), device_id_type=MESH)

    weights = (wq_ref, wk_ref, wv_ref)
    locals_ = [
        pltpu.make_async_copy(x_ref, xall.at[rows_of(me, block)], local_sem.at[0]),
        pltpu.make_async_copy(cot_ref.at[:, lanes(me)], call.at[rows_of(me, block)], local_sem.at[1]),
        pltpu.make_async_copy(omega_ref.at[me], om, local_sem.at[2]),
    ] + [
        pltpu.make_async_copy(
            w.at[:, lanes(me)], wall.at[rows_of(sub, rows), pl.ds(i * head, head)], local_sem.at[3 + i]
        )
        for i, w in enumerate(weights)
    ]
    for copy in locals_:
        copy.start()
    pl.semaphore_wait(barrier, planes + n_sub - 2)

    wcopies = {}
    for i in (1, 2, 0):
        for d in range(1, n_sub):
            wcopies[i, d] = remote(
                weights[i].at[:, lanes(me)],
                wall.at[rows_of(sub, rows), pl.ds(i * head, head)],
                ws.at[i, d - 1], wr.at[i, d - 1], in_column((sub + d) % n_sub),
            )
            wcopies[i, d].start()
    xcopies = [
        remote(x_ref, xall.at[rows_of(me, block)], xs.at[d - 1], xr.at[d - 1], in_plane((me + d) % planes))
        for d in range(1, planes)
    ]
    for copy in xcopies:
        copy.start()
    ccopies = [
        remote(
            cot_ref.at[:, lanes((me + d) % planes)], call.at[rows_of(me, block)],
            cs.at[d - 1], cr.at[d - 1], in_plane((me + d) % planes),
        )
        for d in range(1, planes)
    ]
    for copy in ccopies:
        copy.start()
    for copy in locals_:
        copy.wait()
    for i in (1, 2):
        for d in range(1, n_sub):
            wcopies[i, d].wait()
    for copy in xcopies:
        copy.wait()

    def key_side(b, carry):
        at = rows_of(b, block)
        both = mul(xall[at, :], wall[:, head:], NN)
        key_act = both[:, :head].astype(BF16)
        va[at, :] = both[:, head:].astype(BF16)
        kf[at, :], ks[at, :] = activations(mul(key_act, om[...], NN))
        return carry

    lax.fori_loop(0, planes, key_side, 0)

    def start_sums(a):
        part[a] = acc[a].astype(BF16)
        copies = []
        for d in range(1, n_sub):
            to = (sub + d) % n_sub
            copies.append(remote(
                part.at[a, rows_of(to, piece)], rsin.at[a, d - 1],
                ss.at[a, 0, d - 1], sr.at[a, 0, d - 1], in_column(to),
            ))
            copies.append(remote(
                tot.at[a], totin.at[a, d - 1], ss.at[a, 1, d - 1], sr.at[a, 1, d - 1], in_column(to),
            ))
        for copy in copies:
            copy.start()
        return copies

    def finish_sums(a, copies):
        for copy in copies:
            copy.wait()
        summed = acc[a, rows_of(sub, piece), :]
        total = tot[a]
        for d in range(1, n_sub):
            summed = summed + rsin[a, d - 1].astype(F32)
            total = total + totin[a, d - 1]
        half[a, rows_of(sub, piece), :] = summed.astype(BF16)
        copies = [
            remote(
                half.at[a, rows_of(sub, piece)], half.at[a, rows_of(sub, piece)],
                ss.at[a, 2, d - 1], sr.at[a, 2, d - 1], in_column((sub + d) % n_sub),
            )
            for d in range(1, n_sub)
        ]
        for copy in copies:
            copy.start()
        for copy in copies:
            copy.wait()
        return total

    tot[...] = jnp.zeros_like(tot)
    for r in range(n_grp):
        at = pl.ds(r * record, record)
        acc[0, pl.ds(r * head, head), :] = mul(va[at, :], kf[at, :], TN)
        tot[0, pl.ds(r, 1), :] = jnp.sum(kf[at, :].astype(F32), axis=0, keepdims=True)
    copies = start_sums(0)

    for d in range(1, n_sub):
        wcopies[0, d].wait()

    def query_side(b, carry):
        at = rows_of(b, block)
        queries = mul(xall[at, :], wall[:, :head], NN).astype(BF16)
        qf[at, :], qs[at, :] = activations(mul(queries, om[...], NN))
        return carry

    lax.fori_loop(0, planes, query_side, 0)
    for copy in ccopies:
        copy.wait()
    total = finish_sums(0, copies)
    totals_half = [total[r : r + 1].astype(BF16) for r in range(n_grp)]

    for r in range(n_grp):
        summary = half[0, pl.ds(r * head, head), :]
        wide = jnp.broadcast_to(totals_half[r], summary.shape)
        stacked = jnp.concatenate([summary, wide], axis=0)

        def upstream_side(b, carry, stacked=stacked, r=r):
            at = rows_of(r * n_seq + b, block)
            both = mul(qf[at, :], stacked, NT)
            inverse = 1.0 / both[:, head:]
            attended = both[:, :head] * inverse
            scaled = call[at, :].astype(F32) * loss_scale * inverse
            sc[at, :] = scaled.astype(BF16)
            nrm[at, :] = -jnp.sum(scaled * attended, axis=-1, keepdims=True)
            return carry

        lax.fori_loop(0, n_seq, upstream_side, 0)
        at = pl.ds(r * record, record)
        acc[1, pl.ds(r * head, head), :] = mul(sc[at, :], qf[at, :], TN)
        tot[1, pl.ds(r, 1), :] = jnp.sum(
            qf[at, :].astype(F32) * nrm[at, :].astype(BF16).astype(F32), axis=0, keepdims=True
        )
    copies = start_sums(1)

    for r in range(n_grp):
        def query_grads(b, carry, r=r):
            at = rows_of(r * n_seq + b, block)
            grad = mul(sc[at, :], half[0, pl.ds(r * head, head), :], NN)
            grad = grad + nrm[at, :] * totals_half[r].astype(F32)
            grad = (grad * qs[at, :]).astype(BF16)
            gr[at, pl.ds(0, head)] = mul(grad, om[...], NT).astype(BF16)
            return carry

        lax.fori_loop(0, n_seq, query_grads, 0)
    total_grad = finish_sums(1, copies)

    for r in range(n_grp):
        def key_grads(b, carry, r=r):
            at = rows_of(r * n_seq + b, block)
            summary = half[1, pl.ds(r * head, head), :]
            grad = mul(va[at, :], summary, NN) + total_grad[r : r + 1]
            grad = (grad * ks[at, :]).astype(BF16)
            gr[at, pl.ds(head, head)] = mul(grad, om[...], NT).astype(BF16)
            gr[at, pl.ds(2 * head, head)] = mul(kf[at, :], summary, NT).astype(BF16)
            return carry

        lax.fori_loop(0, n_seq, key_grads, 0)

    def out_copy(d):
        to = (me + d) % planes
        return remote(ob.at[d - 1], oin.at[d - 1], osend.at[d - 1], orecv.at[d - 1], in_plane(to))

    def result(d, carry):
        to = (me + d) % planes
        ob[d - 1] = mul(gr[rows_of(to, block), :], wall[...], NT).astype(BF16)
        out_copy(d).start()
        return carry

    lax.fori_loop(1, planes, result, 0)
    summed = mul(gr[rows_of(me, block), :], wall[...], NT)
    for d in range(1, planes):
        out_copy(d).wait()
        summed = summed + oin[d - 1].astype(F32)
    out_ref[...] = summed.astype(BF16)


def fits(n_grp, n_seq, n_sub, events, offsets, cotangent, query_weight, key_weight, value_weight, omega):
    heads, head, features = omega.shape
    block, width = events.shape
    return (
        heads == n_grp * n_seq and heads > 1 and n_sub > 1 and head % 128 == 0 and features % 128 == 0
        and block % 16 == 0 and n_grp * head % (16 * n_sub) == 0 and query_weight.shape[0] % 16 == 0
        and n_grp <= 8
    )


def fused(n_grp, n_seq, n_sub, events, offsets, cotangent, query_weight, key_weight, value_weight, omega):
    planes = n_grp * n_seq
    block, width = events.shape
    _, head, features = omega.shape
    tokens = planes * block
    piece = n_grp * head // n_sub
    inputs = encode(events, offsets)
    vm = pltpu.VMEM
    dma = pltpu.SemaphoreType.DMA
    scratch = [
        vm((tokens, width), BF16),
        vm((tokens, head), BF16),
        vm((width, 3 * head), BF16),
        vm((head, features), BF16),
        vm((tokens, features), BF16),
        vm((tokens, features), BF16),
        vm((tokens, features), F32),
        vm((tokens, features), F32),
        vm((tokens, head), BF16),
        vm((tokens, head), BF16),
        vm((tokens, 1), F32),
        vm((tokens, 3 * head), BF16),
        vm((2, n_grp * head, features), F32),
        vm((2, n_grp * head, features), BF16),
        vm((2, n_sub - 1, piece, features), BF16),
        vm((2, n_grp * head, features), BF16),
        vm((2, 8, features), F32),
        vm((2, n_sub - 1, 8, features), F32),
        vm((planes - 1, block, width), BF16),
        vm((planes - 1, block, width), BF16),
        dma((6,)),
        dma((planes - 1,)), dma((planes - 1,)),
        dma((planes - 1,)), dma((planes - 1,)),
        dma((3, n_sub - 1)), dma((3, n_sub - 1)),
        dma((2, 3, n_sub - 1)), dma((2, 3, n_sub - 1)),
        dma((planes - 1,)), dma((planes - 1,)),
    ]
    loss_scale = math.sqrt(block * n_seq * n_sub)
    return pl.pallas_call(
        functools.partial(kernel, n_grp, n_seq, n_sub, loss_scale),
        out_shape=jax.ShapeDtypeStruct((block, width), BF16),
        in_specs=[pl.BlockSpec(memory_space=pl.ANY)] * 6,
        out_specs=pl.BlockSpec(memory_space=pltpu.VMEM),
        scratch_shapes=scratch,
        compiler_params=pltpu.CompilerParams(
            collective_id=0, has_side_effects=True, vmem_limit_bytes=48 * 1024 * 1024
        ),
    )(inputs, cotangent, query_weight, key_weight, value_weight, omega)


def solution(mesh):
    in_specs = (
        P(("grp", "seq", "sub"), None),
        P(("grp", "seq", "sub")),
        P(("grp", "seq", "sub"), None),
        P("sub", None),
        P("sub", None),
        P("sub", None),
        P(),
    )
    out_specs = P(("grp", "seq", "sub"), None)
    n_grp, n_seq, n_sub = (mesh.shape[name] for name in ("grp", "seq", "sub"))

    def body(*args):
        if fits(n_grp, n_seq, n_sub, *args):
            return fused(n_grp, n_seq, n_sub, *args)
        return local(*args)

    return jax.shard_map(body, mesh=mesh, in_specs=in_specs, out_specs=out_specs, check_vma=False)
```

```python
import functools
import math

import jax
import jax.numpy as jnp
from jax import lax
from jax.experimental import pallas as pl
from jax.experimental.pallas import tpu as pltpu
from jax.sharding import PartitionSpec as P


def encode(events, offsets):
    half_width = events.shape[1] // 2
    indices = jnp.arange(half_width, dtype=jnp.float32)
    frequency = jnp.exp(indices * (-2.0 * math.log(10000.0) / events.shape[1]))
    angles = offsets.astype(jnp.float32)[:, None] * frequency[None, :]
    encoding = jnp.concatenate([jnp.sin(angles), jnp.cos(angles)], axis=1)
    return (events.astype(jnp.float32) + encoding).astype(jnp.bfloat16)


def split_heads(matrix, head_count):
    return matrix.reshape(matrix.shape[0], head_count, matrix.shape[1] // head_count)


def transposed(left, weight):
    return lax.dot_general(
        left, weight, (((1,), (1,)), ((), ())), preferred_element_type=jnp.float32
    )


def local(events, offsets, cotangent, query_weight, key_weight, value_weight, omega):
    widened_rows = jnp.float32
    head_count = omega.shape[0]
    local_rows = events.shape[0]
    model_width = events.shape[1]
    all_tokens = local_rows * lax.axis_size("seq") * lax.axis_size("sub")
    loss_scale = math.sqrt(all_tokens)
    inputs = encode(events, offsets)
    gathered = (
        lax.all_gather(query_weight, "sub", axis=0, tiled=True),
        lax.all_gather(key_weight, "sub", axis=0, tiled=True),
        lax.all_gather(value_weight, "sub", axis=0, tiled=True),
    )
    queries, key_act, value_act = [
        jnp.dot(inputs, weight, preferred_element_type=widened_rows).astype(jnp.bfloat16)
        for weight in gathered
    ]
    query_pre = jnp.einsum(
        "thd,hdm->thm", split_heads(queries, head_count), omega, preferred_element_type=widened_rows
    )
    key_pre = jnp.einsum(
        "thd,hdm->thm", split_heads(key_act, head_count), omega, preferred_element_type=widened_rows
    )
    query_feature_map = jax.nn.softplus(query_pre).astype(jnp.bfloat16)
    key_feature_map = jax.nn.softplus(key_pre).astype(jnp.bfloat16)
    value_per_head = split_heads(value_act, head_count)
    local_digest = jnp.einsum(
        "reb,rec->ebc", key_feature_map, value_per_head, preferred_element_type=widened_rows
    )
    local_total = jnp.sum(key_feature_map, axis=0, dtype=widened_rows)
    state_digest, key_total = lax.psum((local_digest, local_total), ("seq", "sub"))
    digest_halves = state_digest.astype(jnp.bfloat16)
    total_half = key_total.astype(jnp.bfloat16)
    numerator = jnp.einsum(
        "xls,lsk->xlk", query_feature_map, digest_halves, preferred_element_type=widened_rows
    )
    denom = jnp.einsum(
        "thm,hm->th", query_feature_map, total_half, preferred_element_type=widened_rows
    )
    attended = numerator / denom[..., None]
    upstream = split_heads(cotangent, head_count).astype(widened_rows) * loss_scale
    scaled_grad = upstream / denom[..., None]
    norm_grad = -jnp.sum(scaled_grad * attended, axis=-1)
    scaled_halves = scaled_grad.astype(jnp.bfloat16)
    norm_half = norm_grad.astype(jnp.bfloat16)
    local_gradient = jnp.einsum(
        "reb,rec->ebc", query_feature_map, scaled_halves, preferred_element_type=widened_rows
    )
    local_norm = jnp.einsum(
        "thm,th->hm", query_feature_map, norm_half, preferred_element_type=widened_rows
    )
    summary_grad, overall_gradient = lax.psum((local_gradient, local_norm), ("seq", "sub"))
    gradient_halves = summary_grad.astype(jnp.bfloat16)
    query_feature_gradient = jnp.einsum(
        "pfy,fly->pfl", scaled_halves, digest_halves, preferred_element_type=widened_rows
    )
    query_feature_gradient = (
        query_feature_gradient + norm_grad[..., None] * total_half.astype(widened_rows)[None]
    )
    key_feature_gradient = (
        jnp.einsum(
            "pfy,fly->pfl", value_per_head, gradient_halves, preferred_element_type=widened_rows
        )
        + overall_gradient[None]
    )
    value_gradient = jnp.einsum(
        "xls,lsk->xlk", key_feature_map, gradient_halves, preferred_element_type=widened_rows
    ).astype(jnp.bfloat16)
    query_pre_grad = (query_feature_gradient * jax.nn.sigmoid(query_pre)).astype(jnp.bfloat16)
    key_pre_grad = (key_feature_gradient * jax.nn.sigmoid(key_pre)).astype(jnp.bfloat16)
    query_grad = jnp.einsum(
        "thm,hdm->thd", query_pre_grad, omega, preferred_element_type=widened_rows
    ).astype(jnp.bfloat16)
    key_grad = jnp.einsum(
        "thm,hdm->thd", key_pre_grad, omega, preferred_element_type=widened_rows
    ).astype(jnp.bfloat16)
    query_flat = query_grad.reshape(local_rows, model_width)
    key_flat = key_grad.reshape(local_rows, model_width)
    value_flat = value_gradient.reshape(local_rows, model_width)
    summed = transposed(query_flat, gathered[0])
    summed = summed + transposed(key_flat, gathered[1])
    summed = summed + transposed(value_flat, gathered[2])
    return summed.astype(jnp.bfloat16)


F32, BF16 = jnp.float32, jnp.bfloat16
MESH = pl.DeviceIdType.MESH
NN = (((1,), (0,)), ((), ()))
NT = (((1,), (1,)), ((), ()))
TN = (((0,), (0,)), ((), ()))


def mul(left, right, dims):
    return lax.dot_general(left, right, dims, preferred_element_type=F32)


def activations(pre):
    small = jnp.exp(-jnp.abs(pre))
    feature = jnp.maximum(pre, 0.0) + jnp.log1p(small)
    sigmoid = jnp.where(pre >= 0.0, 1.0, small) / (1.0 + small)
    return feature.astype(BF16), sigmoid


def sin_cos(angle):
    turns = jnp.floor(angle * (2.0 / math.pi) + 0.5)
    rest = ((angle - turns * 1.5703125) - turns * 4.837512969970703125e-4) - turns * 7.54978995489188e-8
    square = rest * rest
    sine = ((-1.9515295891e-4 * square + 8.3321608736e-3) * square - 1.6666654611e-1) * square * rest + rest
    cosine = (
        (2.443315711809948e-5 * square - 1.388731625493765e-3) * square + 4.166664568298827e-2
    ) * square * square - 0.5 * square + 1.0
    quarter = turns.astype(jnp.int32) & 3
    odd = (quarter & 1) == 1
    first = jnp.where(odd, cosine, sine)
    second = jnp.where(odd, sine, cosine)
    first = jnp.where(quarter >= 2, -first, first)
    second = jnp.where((quarter == 1) | (quarter == 2), -second, second)
    return first, second


def kernel(
    n_grp, n_seq, n_sub, loss_scale,
    off_ref, x_ref, cot_ref, wq_ref, wk_ref, wv_ref, omega_ref, out_ref,
    ev, xall, call, wall, om, qf, kf, qs, ks, va, sc, nrm, gr,
    acc, part, rsin, half, tot, totin, pf, ob, oin, sx, sy, rx, ry, s3, r3,
    local_sem, xs, xr, cs, cr, ws, wr, ss, sr, ocs, ocr, o2s, o2r, o3s, o3r,
):
    planes = n_grp * n_seq
    grp, seq, sub = lax.axis_index("grp"), lax.axis_index("seq"), lax.axis_index("sub")
    chip, core = seq // 2, seq % 2
    me = grp * n_seq + seq
    block, width = x_ref.shape
    hb = block // 2
    head = om.shape[0]
    rows = wq_ref.shape[0]
    record = n_seq * block
    piece = head // n_sub

    def place(far_y, far_x, far_core):
        g = 1 - grp if far_y else grp
        x = 1 - chip if far_x else chip
        c = 1 - core if far_core else core
        return g, x * 2 + c

    def pos(*far):
        g, s = place(*far)
        return g * n_seq + s

    def dev(*far):
        g, s = place(*far)
        return {"grp": g, "seq": s, "sub": sub}

    def in_plane(index):
        return {"grp": index // n_seq, "seq": index % n_seq, "sub": sub}

    def in_column(index):
        return {"grp": grp, "seq": seq, "sub": index}

    def rows_of(index, size):
        return pl.ds(pl.multiple_of(index * size, size), size)

    def lanes(index):
        return pl.ds(pl.multiple_of(index * head, head), head)

    def remote(src, dst, send, recv, device):
        return pltpu.make_async_remote_copy(
            src_ref=src, dst_ref=dst, send_sem=send, recv_sem=recv, device_id=device, device_id_type=MESH
        )

    barrier = pltpu.get_barrier_semaphore()
    for d in range(1, planes):
        pl.semaphore_signal(barrier, inc=1, device_id=in_plane((me + d) % planes), device_id_type=MESH)
    for d in range(1, n_sub):
        pl.semaphore_signal(barrier, inc=1, device_id=in_column((sub + d) % n_sub), device_id_type=MESH)

    weights = (wq_ref, wk_ref, wv_ref)
    locals_ = [
        pltpu.make_async_copy(x_ref, ev, local_sem.at[0]),
        pltpu.make_async_copy(cot_ref.at[:, lanes(me)], call.at[rows_of(me, block)], local_sem.at[1]),
        pltpu.make_async_copy(omega_ref.at[me], om, local_sem.at[2]),
    ] + [
        pltpu.make_async_copy(
            w.at[:, lanes(me)], wall.at[rows_of(sub, rows), pl.ds(i * head, head)], local_sem.at[3 + i]
        )
        for i, w in enumerate(weights)
    ]
    for copy in locals_:
        copy.start()

    lane = lax.broadcasted_iota(jnp.int32, (1, width // 2), 1).astype(F32)
    frequency = jnp.exp(lane * (-2.0 * math.log(10000.0) / width))
    offset = jnp.broadcast_to(off_ref[...].astype(F32), (block, block)).T[:, :1]
    sine, cosine = sin_cos(offset * frequency)
    locals_[0].wait()
    own = rows_of(me, block)
    xall[own, : width // 2] = (ev[:, : width // 2].astype(F32) + sine).astype(BF16)
    xall[own, width // 2 :] = (ev[:, width // 2 :].astype(F32) + cosine).astype(BF16)

    pl.semaphore_wait(barrier, planes + n_sub - 2)

    wcopies = {}
    for i in (1, 2, 0):
        for d in range(1, n_sub):
            wcopies[i, d] = remote(
                weights[i].at[:, lanes(me)],
                wall.at[rows_of(sub, rows), pl.ds(i * head, head)],
                ws.at[i, d - 1], wr.at[i, d - 1], in_column((sub + d) % n_sub),
            )

    def xcopy(at, slot, device):
        copy = remote(xall.at[at], xall.at[at], xs.at[slot], xr.at[slot], device)
        copy.start()
        return copy

    to_x, to_y, to_core = dev(0, 1, 0), dev(1, 0, 0), dev(0, 0, 1)
    cx = xcopy(own, 0, to_x)
    cy = xcopy(own, 1, to_y)
    cc = xcopy(own, 2, to_core)
    for copy in wcopies.values():
        copy.start()
    at_x, at_y, at_d = (rows_of(pos(*far), block) for far in ((0, 1, 0), (1, 0, 0), (1, 1, 0)))

    def half_of(index, which):
        return pl.ds(pl.multiple_of(index * block + which * hb, hb), hb)

    cx.wait_recv()
    fy = xcopy(half_of(pos(0, 1, 0), 1), 4, to_y)
    cy.wait_recv()
    fx = xcopy(half_of(pos(1, 0, 0), 0), 3, to_x)
    px = xcopy(at_x, 5, to_core)
    py = xcopy(at_y, 6, to_core)
    ccopies = [
        remote(
            cot_ref.at[:, lanes((me + d) % planes)], call.at[own],
            cs.at[d - 1], cr.at[d - 1], in_plane((me + d) % planes),
        )
        for d in range(1, planes)
    ]
    for copy in ccopies:
        copy.start()
    fx.wait_recv()
    fy.wait_recv()
    pd = xcopy(at_d, 7, to_core)
    for copy in locals_[1:]:
        copy.wait()
    for i in (1, 2):
        for d in range(1, n_sub):
            wcopies[i, d].wait()
    for copy in (cc, px, py, pd):
        copy.wait_recv()
    for copy in (cx, cy, cc, fx, fy, px, py, pd):
        copy.wait_send()

    def start_sums(a, r):
        part[a, r] = acc[a, r].astype(BF16)
        copies = []
        for d in range(1, n_sub):
            to = (sub + d) % n_sub
            copies.append(remote(
                part.at[a, r, rows_of(to, piece)], rsin.at[a, r, d - 1],
                ss.at[a, r, 0, d - 1], sr.at[a, r, 0, d - 1], in_column(to),
            ))
            copies.append(remote(
                tot.at[a, r], totin.at[a, r, d - 1],
                ss.at[a, r, 1, d - 1], sr.at[a, r, 1, d - 1], in_column(to),
            ))
        for copy in copies:
            copy.start()
        return copies

    def spread_sums(a, r, copies):
        for copy in copies:
            copy.wait()
        summed = acc[a, r, rows_of(sub, piece), :]
        total = tot[a, r]
        for d in range(1, n_sub):
            summed = summed + rsin[a, r, d - 1].astype(F32)
            total = total + totin[a, r, d - 1]
        half[a, r, rows_of(sub, piece), :] = summed.astype(BF16)
        copies = [
            remote(
                half.at[a, r, rows_of(sub, piece)], half.at[a, r, rows_of(sub, piece)],
                ss.at[a, r, 2, d - 1], sr.at[a, r, 2, d - 1], in_column((sub + d) % n_sub),
            )
            for d in range(1, n_sub)
        ]
        for copy in copies:
            copy.start()
        return copies, total[:1]

    def wait_all(copies):
        for copy in copies:
            copy.wait()

    def each_block(r, body):
        def step(b, carry):
            body(rows_of(r * n_seq + b, block))
            return carry

        lax.fori_loop(0, n_seq, step, 0)

    def whole(r):
        return pl.ds(r * record, record)

    tot[...] = jnp.zeros_like(tot)

    def key_side(at):
        both = mul(xall[at, :], wall[:, head:], NN)
        key_act = both[:, :head].astype(BF16)
        va[at, :] = both[:, head:].astype(BF16)
        kf[at, :], ks[at, :] = activations(mul(key_act, om[...], NN))

    def query_side(at):
        queries = mul(xall[at, :], wall[:, :head], NN).astype(BF16)
        qf[at, :], qs[at, :] = activations(mul(queries, om[...], NN))

    sums = {}
    records = range(n_grp)
    for r in records:
        each_block(r, key_side)
        acc[0, r] = mul(va[whole(r), :], kf[whole(r), :], TN)
        tot[0, r, pl.ds(0, 1), :] = jnp.sum(kf[whole(r), :].astype(F32), axis=0, keepdims=True)
        sums[r] = start_sums(0, r)
    for d in range(1, n_sub):
        wcopies[0, d].wait()
    spread, totals = {}, {}
    for r in records:
        each_block(r, query_side)
        spread[r], total = spread_sums(0, r, sums[r])
        totals[r] = total.astype(BF16)
    wait_all(ccopies)

    for r in records:
        wait_all(spread[r])
        summary = half[0, r]
        stacked = jnp.concatenate([summary, jnp.broadcast_to(totals[r], summary.shape)], axis=0)

        def upstream_side(at, stacked=stacked):
            both = mul(qf[at, :], stacked, NT)
            inverse = 1.0 / both[:, head:]
            attended = both[:, :head] * inverse
            scaled = call[at, :].astype(F32) * loss_scale * inverse
            sc[at, :] = scaled.astype(BF16)
            nrm[at, :] = -jnp.sum(scaled * attended, axis=-1, keepdims=True)

        each_block(r, upstream_side)
        acc[1, r] = mul(sc[whole(r), :], qf[whole(r), :], TN)
        tot[1, r, pl.ds(0, 1), :] = jnp.sum(
            qf[whole(r), :].astype(F32) * nrm[whole(r), :].astype(BF16).astype(F32), axis=0, keepdims=True
        )
        sums[r] = start_sums(1, r)

    for r in records:
        def query_grads(at, r=r):
            grad = mul(sc[at, :], half[0, r], NN)
            grad = grad + nrm[at, :] * totals[r].astype(F32)
            grad = (grad * qs[at, :]).astype(BF16)
            gr[at, pl.ds(0, head)] = mul(grad, om[...], NT).astype(BF16)

        each_block(r, query_grads)
        spread[r], totals[r] = spread_sums(1, r, sums[r])

    for r in records:
        wait_all(spread[r])

        def key_grads(at, r=r):
            grad = mul(va[at, :], half[1, r], NN) + totals[r]
            grad = (grad * ks[at, :]).astype(BF16)
            gr[at, pl.ds(head, head)] = mul(grad, om[...], NT).astype(BF16)
            gr[at, pl.ds(2 * head, head)] = mul(kf[at, :], half[1, r], NT).astype(BF16)

        each_block(r, key_grads)

    far = ((1, 1), (0, 1), (1, 0), (0, 0))
    to_partner = []
    for t, (fy_, fx_) in enumerate(far):
        ob[t] = mul(gr[rows_of(pos(fy_, fx_, 1), block), :], wall[...], NT).astype(BF16)
        copy = remote(ob.at[t], oin.at[t], ocs.at[t], ocr.at[t], to_core)
        copy.start()
        to_partner.append(copy)
    for t, (fy_, fx_) in enumerate(far):
        pf[t] = mul(gr[rows_of(pos(fy_, fx_, 0), block), :], wall[...], NT)
    top, low = pl.ds(0, hb), pl.ds(hb, hb)

    def send2(buffer, into, i, slot, device):
        copy = remote(buffer.at[i], into.at[i], o2s.at[slot], o2r.at[slot], device)
        copy.start()
        return copy

    to_partner[0].wait()
    sx[0] = (pf[0, top, :] + oin[0, top, :].astype(F32)).astype(BF16)
    x0 = send2(sx, rx, 0, 0, to_x)
    sy[0] = (pf[0, low, :] + oin[0, low, :].astype(F32)).astype(BF16)
    y0 = send2(sy, ry, 0, 1, to_y)
    to_partner[1].wait()
    sx[1] = (pf[1, top, :] + oin[1, top, :].astype(F32)).astype(BF16)
    x1 = send2(sx, rx, 1, 2, to_x)
    to_partner[2].wait()
    sy[1] = (pf[2, low, :] + oin[2, low, :].astype(F32)).astype(BF16)
    y1 = send2(sy, ry, 1, 3, to_y)
    to_partner[3].wait()
    x0.wait()
    s3[0] = (pf[2, top, :] + oin[2, top, :].astype(F32) + rx[0].astype(F32)).astype(BF16)
    z0 = remote(s3.at[0], r3.at[0], o3s.at[0], o3r.at[0], to_y)
    z0.start()
    y0.wait()
    s3[1] = (pf[1, low, :] + oin[1, low, :].astype(F32) + ry[0].astype(F32)).astype(BF16)
    z1 = remote(s3.at[1], r3.at[1], o3s.at[1], o3r.at[1], to_x)
    z1.start()
    x1.wait()
    y1.wait()
    z0.wait()
    out_ref[top, :] = (
        pf[3, top, :] + oin[3, top, :].astype(F32) + rx[1].astype(F32) + r3[0].astype(F32)
    ).astype(BF16)
    z1.wait()
    out_ref[low, :] = (
        pf[3, low, :] + oin[3, low, :].astype(F32) + ry[1].astype(F32) + r3[1].astype(F32)
    ).astype(BF16)


def fits(n_grp, n_seq, n_sub, events, offsets, cotangent, query_weight, key_weight, value_weight, omega):
    heads, head, features = omega.shape
    block, width = events.shape
    return (
        heads == n_grp * n_seq and n_grp == 2 and n_seq == 4 and n_sub > 1 and head % 128 == 0 and features % 128 == 0
        and block % 128 == 0 and head % (16 * n_sub) == 0 and query_weight.shape[0] % 16 == 0 and width % 256 == 0
    )


def fused(n_grp, n_seq, n_sub, events, offsets, cotangent, query_weight, key_weight, value_weight, omega):
    planes = n_grp * n_seq
    block, width = events.shape
    _, head, features = omega.shape
    tokens = planes * block
    piece = head // n_sub
    vm = pltpu.VMEM
    dma = pltpu.SemaphoreType.DMA
    half_block = (2, block // 2, width)
    scratch = [
        vm((block, width), BF16),
        vm((tokens, width), BF16),
        vm((tokens, head), BF16),
        vm((width, 3 * head), BF16),
        vm((head, features), BF16),
        vm((tokens, features), BF16),
        vm((tokens, features), BF16),
        vm((tokens, features), F32),
        vm((tokens, features), F32),
        vm((tokens, head), BF16),
        vm((tokens, head), BF16),
        vm((tokens, 1), F32),
        vm((tokens, 3 * head), BF16),
        vm((2, n_grp, head, features), F32),
        vm((2, n_grp, head, features), BF16),
        vm((2, n_grp, n_sub - 1, piece, features), BF16),
        vm((2, n_grp, head, features), BF16),
        vm((2, n_grp, 8, features), F32),
        vm((2, n_grp, n_sub - 1, 8, features), F32),
        vm((4, block, width), F32),
        vm((4, block, width), BF16),
        vm((4, block, width), BF16),
        vm(half_block, BF16), vm(half_block, BF16), vm(half_block, BF16),
        vm(half_block, BF16), vm(half_block, BF16), vm(half_block, BF16),
        dma((6,)),
        dma((8,)), dma((8,)),
        dma((planes - 1,)), dma((planes - 1,)),
        dma((3, n_sub - 1)), dma((3, n_sub - 1)),
        dma((2, n_grp, 3, n_sub - 1)), dma((2, n_grp, 3, n_sub - 1)),
        dma((4,)), dma((4,)), dma((4,)), dma((4,)), dma((2,)), dma((2,)),
    ]
    loss_scale = math.sqrt(block * n_seq * n_sub)
    return pl.pallas_call(
        functools.partial(kernel, n_grp, n_seq, n_sub, loss_scale),
        out_shape=jax.ShapeDtypeStruct((block, width), BF16),
        in_specs=[pl.BlockSpec(memory_space=pltpu.VMEM)] + [pl.BlockSpec(memory_space=pltpu.HBM)] * 6,
        out_specs=pl.BlockSpec(memory_space=pltpu.VMEM),
        scratch_shapes=scratch,
        compiler_params=pltpu.CompilerParams(
            collective_id=0, has_side_effects=True, vmem_limit_bytes=48 * 1024 * 1024
        ),
    )(offsets.reshape(1, block), events, cotangent, query_weight, key_weight, value_weight, omega)


def solution(mesh):
    in_specs = (
        P(("grp", "seq", "sub"), None),
        P(("grp", "seq", "sub")),
        P(("grp", "seq", "sub"), None),
        P("sub", None),
        P("sub", None),
        P("sub", None),
        P(),
    )
    out_specs = P(("grp", "seq", "sub"), None)
    n_grp, n_seq, n_sub = (mesh.shape[name] for name in ("grp", "seq", "sub"))

    def body(*args):
        if fits(n_grp, n_seq, n_sub, *args):
            return fused(n_grp, n_seq, n_sub, *args)
        return local(*args)

    return jax.shard_map(body, mesh=mesh, in_specs=in_specs, out_specs=out_specs, check_vma=False)
```

```python
import functools
import math

import jax
import jax.numpy as jnp
from jax import lax
from jax.experimental import pallas as pl
from jax.experimental.pallas import tpu as pltpu
from jax.sharding import PartitionSpec as P


def encode(events, offsets):
    half_width = events.shape[1] // 2
    indices = jnp.arange(half_width, dtype=jnp.float32)
    frequency = jnp.exp(indices * (-2.0 * math.log(10000.0) / events.shape[1]))
    angles = offsets.astype(jnp.float32)[:, None] * frequency[None, :]
    encoding = jnp.concatenate([jnp.sin(angles), jnp.cos(angles)], axis=1)
    return (events.astype(jnp.float32) + encoding).astype(jnp.bfloat16)


def split_heads(matrix, head_count):
    return matrix.reshape(matrix.shape[0], head_count, matrix.shape[1] // head_count)


def transposed(left, weight):
    return lax.dot_general(
        left, weight, (((1,), (1,)), ((), ())), preferred_element_type=jnp.float32
    )


def local(events, offsets, cotangent, query_weight, key_weight, value_weight, omega):
    widened_rows = jnp.float32
    head_count = omega.shape[0]
    local_rows = events.shape[0]
    model_width = events.shape[1]
    all_tokens = local_rows * lax.axis_size("seq") * lax.axis_size("sub")
    loss_scale = math.sqrt(all_tokens)
    inputs = encode(events, offsets)
    gathered = (
        lax.all_gather(query_weight, "sub", axis=0, tiled=True),
        lax.all_gather(key_weight, "sub", axis=0, tiled=True),
        lax.all_gather(value_weight, "sub", axis=0, tiled=True),
    )
    queries, key_act, value_act = [
        jnp.dot(inputs, weight, preferred_element_type=widened_rows).astype(jnp.bfloat16)
        for weight in gathered
    ]
    query_pre = jnp.einsum(
        "thd,hdm->thm", split_heads(queries, head_count), omega, preferred_element_type=widened_rows
    )
    key_pre = jnp.einsum(
        "thd,hdm->thm", split_heads(key_act, head_count), omega, preferred_element_type=widened_rows
    )
    query_feature_map = jax.nn.softplus(query_pre).astype(jnp.bfloat16)
    key_feature_map = jax.nn.softplus(key_pre).astype(jnp.bfloat16)
    value_per_head = split_heads(value_act, head_count)
    local_digest = jnp.einsum(
        "reb,rec->ebc", key_feature_map, value_per_head, preferred_element_type=widened_rows
    )
    local_total = jnp.sum(key_feature_map, axis=0, dtype=widened_rows)
    state_digest, key_total = lax.psum((local_digest, local_total), ("seq", "sub"))
    digest_halves = state_digest.astype(jnp.bfloat16)
    total_half = key_total.astype(jnp.bfloat16)
    numerator = jnp.einsum(
        "xls,lsk->xlk", query_feature_map, digest_halves, preferred_element_type=widened_rows
    )
    denom = jnp.einsum(
        "thm,hm->th", query_feature_map, total_half, preferred_element_type=widened_rows
    )
    attended = numerator / denom[..., None]
    upstream = split_heads(cotangent, head_count).astype(widened_rows) * loss_scale
    scaled_grad = upstream / denom[..., None]
    norm_grad = -jnp.sum(scaled_grad * attended, axis=-1)
    scaled_halves = scaled_grad.astype(jnp.bfloat16)
    norm_half = norm_grad.astype(jnp.bfloat16)
    local_gradient = jnp.einsum(
        "reb,rec->ebc", query_feature_map, scaled_halves, preferred_element_type=widened_rows
    )
    local_norm = jnp.einsum(
        "thm,th->hm", query_feature_map, norm_half, preferred_element_type=widened_rows
    )
    summary_grad, overall_gradient = lax.psum((local_gradient, local_norm), ("seq", "sub"))
    gradient_halves = summary_grad.astype(jnp.bfloat16)
    query_feature_gradient = jnp.einsum(
        "pfy,fly->pfl", scaled_halves, digest_halves, preferred_element_type=widened_rows
    )
    query_feature_gradient = (
        query_feature_gradient + norm_grad[..., None] * total_half.astype(widened_rows)[None]
    )
    key_feature_gradient = (
        jnp.einsum(
            "pfy,fly->pfl", value_per_head, gradient_halves, preferred_element_type=widened_rows
        )
        + overall_gradient[None]
    )
    value_gradient = jnp.einsum(
        "xls,lsk->xlk", key_feature_map, gradient_halves, preferred_element_type=widened_rows
    ).astype(jnp.bfloat16)
    query_pre_grad = (query_feature_gradient * jax.nn.sigmoid(query_pre)).astype(jnp.bfloat16)
    key_pre_grad = (key_feature_gradient * jax.nn.sigmoid(key_pre)).astype(jnp.bfloat16)
    query_grad = jnp.einsum(
        "thm,hdm->thd", query_pre_grad, omega, preferred_element_type=widened_rows
    ).astype(jnp.bfloat16)
    key_grad = jnp.einsum(
        "thm,hdm->thd", key_pre_grad, omega, preferred_element_type=widened_rows
    ).astype(jnp.bfloat16)
    query_flat = query_grad.reshape(local_rows, model_width)
    key_flat = key_grad.reshape(local_rows, model_width)
    value_flat = value_gradient.reshape(local_rows, model_width)
    summed = transposed(query_flat, gathered[0])
    summed = summed + transposed(key_flat, gathered[1])
    summed = summed + transposed(value_flat, gathered[2])
    return summed.astype(jnp.bfloat16)


F32, BF16 = jnp.float32, jnp.bfloat16
MESH = pl.DeviceIdType.MESH
NN = (((1,), (0,)), ((), ()))
NT = (((1,), (1,)), ((), ()))
TN = (((0,), (0,)), ((), ()))


def mul(left, right, dims):
    return lax.dot_general(left, right, dims, preferred_element_type=F32)


def activations(pre):
    small = jnp.exp(-jnp.abs(pre))
    feature = jnp.maximum(pre, 0.0) + jnp.log1p(small)
    sigmoid = jnp.where(pre >= 0.0, 1.0, small) / (1.0 + small)
    return feature.astype(BF16), sigmoid


def sin_cos(angle):
    turns = jnp.floor(angle * (2.0 / math.pi) + 0.5)
    rest = ((angle - turns * 1.5703125) - turns * 4.837512969970703125e-4) - turns * 7.54978995489188e-8
    square = rest * rest
    sine = ((-1.9515295891e-4 * square + 8.3321608736e-3) * square - 1.6666654611e-1) * square * rest + rest
    cosine = (
        (2.443315711809948e-5 * square - 1.388731625493765e-3) * square + 4.166664568298827e-2
    ) * square * square - 0.5 * square + 1.0
    quarter = turns.astype(jnp.int32) & 3
    odd = (quarter & 1) == 1
    first = jnp.where(odd, cosine, sine)
    second = jnp.where(odd, sine, cosine)
    first = jnp.where(quarter >= 2, -first, first)
    second = jnp.where((quarter == 1) | (quarter == 2), -second, second)
    return first, second


def kernel(
    n_grp, n_seq, n_sub, loss_scale,
    off_ref, x_ref, cot_ref, wq_ref, wk_ref, wv_ref, omega_ref, out_ref,
    ev, xall, call, wall, om, qf, kf, qs, ks, va, sc, nrm, gr,
    acc, part, rsin, half, tot, totin, pf, ob, oin, sx, sy, rx, ry, s3, r3,
    local_sem, xs, xr, cs, cr, qws, qwr, ws, wr, ss, sr, ocs, ocr, o2s, o2r, o3s, o3r,
):
    planes = n_grp * n_seq
    grp, seq, sub = lax.axis_index("grp"), lax.axis_index("seq"), lax.axis_index("sub")
    chip, core = seq // 2, seq % 2
    me = grp * n_seq + seq
    block, width = x_ref.shape
    hb = block // 2
    head = om.shape[0]
    rows = wq_ref.shape[0]
    record = n_seq * block
    piece = head // n_sub

    def place(far_y, far_x, far_core):
        g = 1 - grp if far_y else grp
        x = 1 - chip if far_x else chip
        c = 1 - core if far_core else core
        return g, x * 2 + c

    def pos(*far):
        g, s = place(*far)
        return g * n_seq + s

    def dev(*far):
        g, s = place(*far)
        return {"grp": g, "seq": s, "sub": sub}

    def in_plane(index):
        return {"grp": index // n_seq, "seq": index % n_seq, "sub": sub}

    def in_column(index):
        return {"grp": grp, "seq": seq, "sub": index}

    def rows_of(index, size):
        return pl.ds(pl.multiple_of(index * size, size), size)

    def lanes(index):
        return pl.ds(pl.multiple_of(index * head, head), head)

    def remote(src, dst, send, recv, device):
        return pltpu.make_async_remote_copy(
            src_ref=src, dst_ref=dst, send_sem=send, recv_sem=recv, device_id=device, device_id_type=MESH
        )

    barrier = pltpu.get_barrier_semaphore()
    for d in range(1, planes):
        pl.semaphore_signal(barrier, inc=1, device_id=in_plane((me + d) % planes), device_id_type=MESH)
    for d in range(1, n_sub):
        pl.semaphore_signal(barrier, inc=1, device_id=in_column((sub + d) % n_sub), device_id_type=MESH)

    weights = (wq_ref, wk_ref, wv_ref)
    locals_ = [
        pltpu.make_async_copy(x_ref, ev, local_sem.at[0]),
        pltpu.make_async_copy(cot_ref.at[:, lanes(me)], call.at[rows_of(me, block)], local_sem.at[1]),
        pltpu.make_async_copy(omega_ref.at[me], om, local_sem.at[2]),
    ] + [
        pltpu.make_async_copy(
            w.at[:, lanes(me)], wall.at[rows_of(sub, rows), pl.ds(i * head, head)], local_sem.at[3 + i]
        )
        for i, w in enumerate(weights)
    ]
    for copy in locals_:
        copy.start()

    lane = lax.broadcasted_iota(jnp.int32, (1, width // 2), 1).astype(F32)
    frequency = jnp.exp(lane * (-2.0 * math.log(10000.0) / width))
    offset = jnp.broadcast_to(off_ref[...].astype(F32), (block, block)).T[:, :1]
    sine, cosine = sin_cos(offset * frequency)
    locals_[0].wait()
    own = rows_of(me, block)
    xall[own, : width // 2] = (ev[:, : width // 2].astype(F32) + sine).astype(BF16)
    xall[own, width // 2 :] = (ev[:, width // 2 :].astype(F32) + cosine).astype(BF16)

    pl.semaphore_wait(barrier, planes + n_sub - 2)

    qcopies = [
        remote(
            wq_ref.at[:, lanes(me)], wall.at[rows_of(sub, rows), pl.ds(0, head)],
            qws.at[d - 1], qwr.at[d - 1], in_column((sub + d) % n_sub),
        )
        for d in range(1, n_sub)
    ]
    both_ways = (0, 1)
    steps = n_sub - 1

    def passed(step, way):
        owner, target = (sub - step, sub + 1) if way else (sub + step, sub - 1)
        at = wall.at[rows_of(owner, rows), pl.ds(head, 2 * head)]
        copy = remote(at, at, ws.at[way, step], wr.at[way, step], in_column(target))
        return copy, ((owner >= 0) & (target < n_sub) if way else (owner < n_sub) & (target >= 0))

    def pass_on(step):
        for way in both_ways:
            copy, active = passed(step, way)
            pl.when(active)(copy.start)

    def sent(step):
        for way in both_ways:
            copy, active = passed(step, way)
            pl.when(active)(copy.wait_send)

    def arrived(step):
        for way in both_ways:
            at = wall.at[rows_of(sub, rows), pl.ds(head, 2 * head)]
            copy = remote(at, at, ws.at[way, step], wr.at[way, step], in_column((sub + 1) % n_sub))
            pl.when(sub >= step + 1 if way else sub + 1 + step < n_sub)(copy.wait_recv)

    def xcopy(at, slot, device):
        copy = remote(xall.at[at], xall.at[at], xs.at[slot], xr.at[slot], device)
        copy.start()
        return copy

    to_x, to_y, to_core = dev(0, 1, 0), dev(1, 0, 0), dev(0, 0, 1)
    cx = xcopy(own, 0, to_x)
    cy = xcopy(own, 1, to_y)
    cc = xcopy(own, 2, to_core)
    locals_[4].wait()
    locals_[5].wait()
    pass_on(0)
    at_x, at_y, at_d = (rows_of(pos(*far), block) for far in ((0, 1, 0), (1, 0, 0), (1, 1, 0)))

    def half_of(index, which):
        return pl.ds(pl.multiple_of(index * block + which * hb, hb), hb)

    if steps > 1:
        arrived(0)
        pass_on(1)
    cx.wait_recv()
    fy = xcopy(half_of(pos(0, 1, 0), 1), 4, to_y)
    cy.wait_recv()
    fx = xcopy(half_of(pos(1, 0, 0), 0), 3, to_x)
    px = xcopy(at_x, 5, to_core)
    py = xcopy(at_y, 6, to_core)
    for step in range(2, steps):
        arrived(step - 1)
        pass_on(step)
    for copy in qcopies:
        copy.start()
    ccopies = [
        remote(
            cot_ref.at[:, lanes((me + d) % planes)], call.at[own],
            cs.at[d - 1], cr.at[d - 1], in_plane((me + d) % planes),
        )
        for d in range(1, planes)
    ]
    for copy in ccopies:
        copy.start()
    for copy in locals_[1:4]:
        copy.wait()
    arrived(steps - 1)
    cc.wait_recv()
    px.wait_recv()

    def start_sums(a, r):
        part[a, r] = acc[a, r].astype(BF16)
        copies = []
        for d in range(1, n_sub):
            to = (sub + d) % n_sub
            copies.append(remote(
                part.at[a, r, rows_of(to, piece)], rsin.at[a, r, d - 1],
                ss.at[a, r, 0, d - 1], sr.at[a, r, 0, d - 1], in_column(to),
            ))
            copies.append(remote(
                tot.at[a, r], totin.at[a, r, d - 1],
                ss.at[a, r, 1, d - 1], sr.at[a, r, 1, d - 1], in_column(to),
            ))
        for copy in copies:
            copy.start()
        return copies

    def spread_sums(a, r, copies):
        for copy in copies:
            copy.wait()
        summed = acc[a, r, rows_of(sub, piece), :]
        total = tot[a, r]
        for d in range(1, n_sub):
            summed = summed + rsin[a, r, d - 1].astype(F32)
            total = total + totin[a, r, d - 1]
        half[a, r, rows_of(sub, piece), :] = summed.astype(BF16)
        copies = [
            remote(
                half.at[a, r, rows_of(sub, piece)], half.at[a, r, rows_of(sub, piece)],
                ss.at[a, r, 2, d - 1], sr.at[a, r, 2, d - 1], in_column((sub + d) % n_sub),
            )
            for d in range(1, n_sub)
        ]
        for copy in copies:
            copy.start()
        return copies, total[:1]

    def wait_all(copies):
        for copy in copies:
            copy.wait()

    def whole(r):
        return rows_of(r, record)

    def wide_norm(at):
        return jnp.concatenate([nrm[at, :]] * (om.shape[1] // head), axis=1)


    def key_side(at):
        both = mul(xall[at, :], wall[:, head:], NN)
        key_act = both[:, :head].astype(BF16)
        va[at, :] = both[:, head:].astype(BF16)
        kf[at, :], ks[at, :] = activations(mul(key_act, om[...], NN))

    def query_side(at):
        queries = mul(xall[at, :], wall[:, :head], NN).astype(BF16)
        qf[at, :], qs[at, :] = activations(mul(queries, om[...], NN))

    sums, spread, totals = {}, {}, {}
    order = (grp, 1 - grp)
    for i, r in enumerate(order):
        key_side(whole(r))
        acc[0, r] = mul(va[whole(r), :], kf[whole(r), :], TN)
        tot[0, r] = jnp.sum(kf[whole(r), :].astype(F32), axis=0, keepdims=True)
        sums[i] = start_sums(0, r)
        if i == 0:
            fx.wait_recv()
            fy.wait_recv()
            pd = xcopy(at_d, 7, to_core)
            py.wait_recv()
            pd.wait_recv()
    for copy in (cx, cy, cc, fx, fy, px, py, pd):
        copy.wait_send()
    for step in range(steps):
        sent(step)
    for copy in qcopies:
        copy.wait()
    for i, r in enumerate(order):
        query_side(whole(r))
        spread[i], total = spread_sums(0, r, sums[i])
        totals[i] = total.astype(BF16)
    wait_all(ccopies)

    for i, r in enumerate(order):
        wait_all(spread[i])
        at = whole(r)
        summary = half[0, r]
        stacked = jnp.concatenate([summary, jnp.broadcast_to(totals[i], summary.shape)], axis=0)
        both = mul(qf[at, :], stacked, NT)
        inverse = 1.0 / both[:, head:]
        attended = both[:, :head] * inverse
        scaled = call[at, :].astype(F32) * loss_scale * inverse
        sc[at, :] = scaled.astype(BF16)
        nrm[at, :] = jnp.broadcast_to(-jnp.sum(scaled * attended, axis=-1, keepdims=True), scaled.shape)
        acc[1, r] = mul(sc[at, :], qf[at, :], TN)
        tot[1, r] = jnp.sum(
            qf[at, :].astype(F32) * wide_norm(at).astype(BF16).astype(F32), axis=0, keepdims=True
        )
        sums[i] = start_sums(1, r)

    for i, r in enumerate(order):
        at = whole(r)
        grad = mul(sc[at, :], half[0, r], NN)
        grad = grad + wide_norm(at) * totals[i].astype(F32)
        grad = (grad * qs[at, :]).astype(BF16)
        gr[at, pl.ds(0, head)] = mul(grad, om[...], NT).astype(BF16)
        spread[i], totals[i] = spread_sums(1, r, sums[i])

    far = ((1, 1), (0, 1), (1, 0), (0, 0))
    to_partner = {}
    for i, r in enumerate(order):
        wait_all(spread[i])
        at = whole(r)
        grad = mul(va[at, :], half[1, r], NN) + totals[i]
        grad = (grad * ks[at, :]).astype(BF16)
        gr[at, pl.ds(head, head)] = mul(grad, om[...], NT).astype(BF16)
        gr[at, pl.ds(2 * head, head)] = mul(kf[at, :], half[1, r], NT).astype(BF16)
        mine = [t for t in range(4) if far[t][0] == i]
        for t in mine:
            ob[t] = mul(gr[rows_of(pos(*far[t], 1), block), :], wall[...], NT).astype(BF16)
            to_partner[t] = remote(ob.at[t], oin.at[t], ocs.at[t], ocr.at[t], to_core)
            to_partner[t].start()
        for t in mine:
            pf[t] = mul(gr[rows_of(pos(*far[t], 0), block), :], wall[...], NT)
        if i == 0:
            to_partner[1].wait()
            sx[1] = (pf[1, pl.ds(0, hb), :] + oin[1, pl.ds(0, hb), :].astype(F32)).astype(BF16)
            x1 = remote(sx.at[1], rx.at[1], o2s.at[2], o2r.at[2], to_x)
            x1.start()
    top, low = pl.ds(0, hb), pl.ds(hb, hb)

    def send2(buffer, into, i, slot, device):
        copy = remote(buffer.at[i], into.at[i], o2s.at[slot], o2r.at[slot], device)
        copy.start()
        return copy

    to_partner[0].wait()
    sx[0] = (pf[0, top, :] + oin[0, top, :].astype(F32)).astype(BF16)
    x0 = send2(sx, rx, 0, 0, to_x)
    sy[0] = (pf[0, low, :] + oin[0, low, :].astype(F32)).astype(BF16)
    y0 = send2(sy, ry, 0, 1, to_y)
    to_partner[2].wait()
    sy[1] = (pf[2, low, :] + oin[2, low, :].astype(F32)).astype(BF16)
    y1 = send2(sy, ry, 1, 3, to_y)
    to_partner[3].wait()
    x0.wait()
    s3[0] = (pf[2, top, :] + oin[2, top, :].astype(F32) + rx[0].astype(F32)).astype(BF16)
    z0 = remote(s3.at[0], r3.at[0], o3s.at[0], o3r.at[0], to_y)
    z0.start()
    y0.wait()
    s3[1] = (pf[1, low, :] + oin[1, low, :].astype(F32) + ry[0].astype(F32)).astype(BF16)
    z1 = remote(s3.at[1], r3.at[1], o3s.at[1], o3r.at[1], to_x)
    z1.start()
    x1.wait()
    y1.wait()
    z0.wait()
    out_ref[top, :] = (
        pf[3, top, :] + oin[3, top, :].astype(F32) + rx[1].astype(F32) + r3[0].astype(F32)
    ).astype(BF16)
    z1.wait()
    out_ref[low, :] = (
        pf[3, low, :] + oin[3, low, :].astype(F32) + ry[1].astype(F32) + r3[1].astype(F32)
    ).astype(BF16)


def fits(n_grp, n_seq, n_sub, events, offsets, cotangent, query_weight, key_weight, value_weight, omega):
    heads, head, features = omega.shape
    block, width = events.shape
    return (
        heads == n_grp * n_seq and n_grp == 2 and n_seq == 4 and n_sub > 1 and head % 128 == 0 and features % head == 0
        and block % 128 == 0 and head % (16 * n_sub) == 0 and query_weight.shape[0] % 16 == 0 and width % 256 == 0
    )


def fused(n_grp, n_seq, n_sub, events, offsets, cotangent, query_weight, key_weight, value_weight, omega):
    planes = n_grp * n_seq
    block, width = events.shape
    _, head, features = omega.shape
    tokens = planes * block
    piece = head // n_sub
    vm = pltpu.VMEM
    dma = pltpu.SemaphoreType.DMA
    half_block = (2, block // 2, width)
    scratch = [
        vm((block, width), BF16),
        vm((tokens, width), BF16),
        vm((tokens, head), BF16),
        vm((width, 3 * head), BF16),
        vm((head, features), BF16),
        vm((tokens, features), BF16),
        vm((tokens, features), BF16),
        vm((tokens, features), F32),
        vm((tokens, features), F32),
        vm((tokens, head), BF16),
        vm((tokens, head), BF16),
        vm((tokens, head), F32),
        vm((tokens, 3 * head), BF16),
        vm((2, n_grp, head, features), F32),
        vm((2, n_grp, head, features), BF16),
        vm((2, n_grp, n_sub - 1, piece, features), BF16),
        vm((2, n_grp, head, features), BF16),
        vm((2, n_grp, 1, features), F32),
        vm((2, n_grp, n_sub - 1, 1, features), F32),
        vm((4, block, width), F32),
        vm((4, block, width), BF16),
        vm((4, block, width), BF16),
        vm(half_block, BF16), vm(half_block, BF16), vm(half_block, BF16),
        vm(half_block, BF16), vm(half_block, BF16), vm(half_block, BF16),
        dma((6,)),
        dma((8,)), dma((8,)),
        dma((planes - 1,)), dma((planes - 1,)),
        dma((n_sub - 1,)), dma((n_sub - 1,)),
        dma((2, n_sub - 1)), dma((2, n_sub - 1)),
        dma((2, n_grp, 3, n_sub - 1)), dma((2, n_grp, 3, n_sub - 1)),
        dma((4,)), dma((4,)), dma((4,)), dma((4,)), dma((2,)), dma((2,)),
    ]
    loss_scale = math.sqrt(block * n_seq * n_sub)
    return pl.pallas_call(
        functools.partial(kernel, n_grp, n_seq, n_sub, loss_scale),
        out_shape=jax.ShapeDtypeStruct((block, width), BF16),
        in_specs=[pl.BlockSpec(memory_space=pltpu.VMEM)] + [pl.BlockSpec(memory_space=pltpu.HBM)] * 6,
        out_specs=pl.BlockSpec(memory_space=pltpu.VMEM),
        scratch_shapes=scratch,
        compiler_params=pltpu.CompilerParams(
            collective_id=0, has_side_effects=True
        ),
    )(offsets.reshape(1, block), events, cotangent, query_weight, key_weight, value_weight, omega)


def solution(mesh):
    in_specs = (
        P(("grp", "seq", "sub"), None),
        P(("grp", "seq", "sub")),
        P(("grp", "seq", "sub"), None),
        P("sub", None),
        P("sub", None),
        P("sub", None),
        P(),
    )
    out_specs = P(("grp", "seq", "sub"), None)
    n_grp, n_seq, n_sub = (mesh.shape[name] for name in ("grp", "seq", "sub"))

    def body(*args):
        if fits(n_grp, n_seq, n_sub, *args):
            return fused(n_grp, n_seq, n_sub, *args)
        return local(*args)

    return jax.shard_map(body, mesh=mesh, in_specs=in_specs, out_specs=out_specs, check_vma=False)
```
